32 devices in a mesh: freq: 4 (over x, core), tm: 8 (over z, y).
Axes of the slice: x: 2, y: 2, z: 4, core: 2. Of those that a mesh axis runs over, the one named last changes fastest.
Arguments:
- visibilities: float32 [8, 8, 1024], P('freq', None, 'tm'), may hold values from -6 to 6
- coherencies: bfloat16 [8, 8, 8, 1024], P('freq', None, None, 'tm'), may hold values from -2.09375 to 2.09375
- pairs: int32 [2, 1024], P(None, 'tm'), may hold values from 0 to 511, as said below
- gains_start: float32 [8, 8, 8, 512], P('freq'), may hold values from -0.9 to 1.9
- duals_start: float32 [8, 8, 8, 512], P('freq'), may hold values from -12 to 12
- poly_start: float32 [4, 8, 8, 512], replicated, may hold values from -0.6 to 1.6
Outputs:
- gains: float32 [8, 8, 8, 512], P('freq')
- duals: float32 [8, 8, 8, 512], P('freq')
- polynomial: float32 [4, 8, 8, 512], replicated
The draws below stay inside these ranges and needn't reach their ends.
Inputs may be any that keep to these rules, and one draw needn't show every extreme that they name: `pairs`: each row names two different stations.
All inputs are finite; a program needn't handle non-finite values.
Results may differ from the reference program's by a relative error of at most 0.0003.
Values sent between devices are 32-bit elements; how exact they have to be, the bound alone decides.
A program may use at most 64 MiB of HBM per device.

```python
from functools import partial
import jax
import jax.numpy as jnp
from jax import lax

STATIONS = 512
DIRS = 8
POLY = 4
ITERS = 2
STEPS = 1
NCHAN = 8
ROWS_ALL = 1024


def identity_mask():
    index = jnp.arange(8)
    return ((index == 0) | (index == 3)).astype(jnp.float32)[None, :, None, None]


def draw_pairs(key, part):
    first_key, second_key = jax.random.split(jax.random.fold_in(key, 11))
    first = jax.random.randint(first_key, (ROWS_ALL,), 0, STATIONS)
    offset = jax.random.randint(second_key, (ROWS_ALL,), 1, STATIONS)
    second = (first + offset) % STATIONS
    return jnp.stack([first, second]).astype(jnp.int32)


def draw_gains_start(key, part):
    noise_key = jax.random.fold_in(jax.random.fold_in(key, 23), 0)
    shape = (NCHAN, 8, DIRS, STATIONS)
    noise = 0.3 * jnp.clip(jax.random.normal(noise_key, shape, jnp.float32), -3.0, 3.0)
    return noise + identity_mask()


def draw_poly_start(key, part):
    noise_key = jax.random.fold_in(jax.random.fold_in(key, 37), 0)
    shape = (POLY, 8, DIRS, STATIONS)
    noise = 0.2 * jnp.clip(jax.random.normal(noise_key, shape, jnp.float32), -3.0, 3.0)
    leading = (jnp.arange(POLY) == 0).astype(jnp.float32)[:, None, None, None]
    return noise + leading * identity_mask()


def block_levels(own_key, extent, pieces, low, largest):
    def one(dim, shards_of):
        heights = jax.random.uniform(jax.random.fold_in(jax.random.fold_in(own_key, 6), dim), (shards_of,), jnp.float32, low / len(pieces), largest / len(pieces))
        return jnp.repeat(jnp.exp(heights), extent[dim] // shards_of).reshape((-1,) + (1,) * (len(extent) - dim - 1))

    gain = one(*pieces[0])
    for cut in pieces[1:]:
        gain = gain * one(*cut)
    return gain


def normal_values(stream_key, dims, scale, most, cuts=(), kind=jnp.bfloat16):
    entries = jax.random.normal(stream_key, dims, jnp.float32) * scale
    if len(cuts) > 0:
        entries = block_levels(stream_key, dims, cuts, -0.22, 0.18) * entries
    return jnp.clip(entries, min=-most, max=most).astype(kind)


def setup_inputs(seed: int = 0) -> dict:
    splits = jax.random.split(jax.random.key(seed), 7)
    return {
        "visibilities": normal_values(splits[0], (NCHAN, 8, ROWS_ALL), 1.0, 6.0, ((0, 4), (2, 8)), jnp.float32),
        "coherencies": normal_values(splits[1], (NCHAN, 8, DIRS, ROWS_ALL), 0.35, 2.09375, ((0, 4), (3, 8))),
        "pairs": draw_pairs(jax.random.fold_in(splits[6], 71), 0),
        "gains_start": draw_gains_start(jax.random.fold_in(splits[6], 71), 0),
        "duals_start": normal_values(splits[4], (NCHAN, 8, DIRS, STATIONS), 2.0, 12.0, ((0, 4),), jnp.float32),
        "poly_start": draw_poly_start(jax.random.fold_in(splits[6], 71), 0),
    }


RHO = 16.0
HIGHEST = lax.Precision.HIGHEST

def split(block):
    return ([block[i] for i in range(4)], [block[i + 4] for i in range(4)])

def join(matrix):
    return jnp.stack(matrix[0] + matrix[1])

def adjoint(matrix):
    real_part, imag_part = matrix
    return ([real_part[0], real_part[2], real_part[1], real_part[3]], [-imag_part[0], -imag_part[2], -imag_part[1], -imag_part[3]])

def product(left, right):
    left_real, left_imag = left
    right_real, right_imag = right
    out_real = []
    out_imag = []
    for row in range(2):
        for column in range(2):
            first = 2 * row
            out_real.append(left_real[first] * right_real[column] - left_imag[first] * right_imag[column] + left_real[first + 1] * right_real[column + 2] - left_imag[first + 1] * right_imag[column + 2])
            out_imag.append(left_real[first] * right_imag[column] + left_imag[first] * right_real[column] + left_real[first + 1] * right_imag[column + 2] + left_imag[first + 1] * right_real[column + 2])
    return (out_real, out_imag)

def normal(matrix):
    real_part, imag_part = matrix
    top_left = real_part[0] ** 2 + imag_part[0] ** 2 + real_part[1] ** 2 + imag_part[1] ** 2
    bottom_right = real_part[2] ** 2 + imag_part[2] ** 2 + real_part[3] ** 2 + imag_part[3] ** 2
    cross_real = real_part[0] * real_part[2] + imag_part[0] * imag_part[2] + real_part[1] * real_part[3] + imag_part[1] * imag_part[3]
    cross_imag = imag_part[0] * real_part[2] - real_part[0] * imag_part[2] + imag_part[1] * real_part[3] - real_part[1] * imag_part[3]
    return jnp.stack([top_left, bottom_right, cross_real, cross_imag])

def data_sums(gains, coherencies, visibilities, pairs):
    jones_first = split(jnp.take(gains, pairs[0], axis=2))
    jones_second = split(jnp.take(gains, pairs[1], axis=2))
    skymodel = split(coherencies.astype(jnp.float32))
    left = product(jones_first, skymodel)
    right = product(skymodel, adjoint(jones_second))
    model = jnp.sum(join(product(left, adjoint(jones_second))), axis=1)
    residual = split((visibilities - model)[:, None, :])
    first_terms = jnp.concatenate([join(product(residual, adjoint(right))), normal(right)], axis=0)
    second_terms = jnp.concatenate([join(product(adjoint(residual), left)), normal(adjoint(left))], axis=0)
    terms = jnp.concatenate([first_terms, second_terms], axis=2)
    stations = jnp.concatenate([pairs[0], pairs[1]]).astype(jnp.int32)
    flat = terms.reshape(-1, terms.shape[2]).T
    summed = jax.ops.segment_sum(flat, stations, num_segments=gains.shape[2])
    return summed.T.reshape(12, gains.shape[1], gains.shape[2])

def update(gains, duals, prior, sums, damping):
    direction = split(sums[:8] - duals - RHO * (gains - prior))
    top_left, bottom_right, cross_real, cross_imag = (sums[8], sums[9], sums[10], sums[11])
    shift = damping * 0.5 * (top_left + bottom_right) + RHO
    upper = top_left + shift
    lower = bottom_right + shift
    determinant = upper * lower - cross_real * cross_real - cross_imag * cross_imag
    zeros = jnp.zeros_like(determinant)
    inverse = ([lower / determinant, -cross_real / determinant, -cross_real / determinant, upper / determinant], [zeros, -cross_imag / determinant, cross_imag / determinant, zeros])
    return gains + join(product(direction, inverse))

def basis_weights(count):
    position = (2.0 * jnp.arange(count).astype(jnp.float32) + 1.0) / count - 1.0
    basis = jnp.stack([jnp.ones_like(position), position, 1.5 * position * position - 0.5, 2.5 * position * position * position - 1.5 * position], axis=1)
    gram = jnp.dot(basis.T, basis, precision=HIGHEST)
    factor = jnp.linalg.cholesky(gram)
    weights = jax.scipy.linalg.cho_solve((factor, True), basis.T)
    return (basis, weights)

def reference(visibilities, coherencies, pairs, gains_start, duals_start, poly_start):
    basis, weights = basis_weights(gains_start.shape[0])
    prior = jnp.einsum('fj,jcks->fcks', basis, poly_start, precision=HIGHEST)
    gains, duals, polynomial = (gains_start, duals_start, poly_start)

    def channel(items):
        return data_sums(items[0], items[1], items[2], pairs)
    for outer in range(STEPS):
        for inner in range(ITERS):
            sums = lax.map(channel, (gains, coherencies, visibilities))
            gains = jax.vmap(partial(update, damping=12.0 * 0.5 ** inner))(gains, duals, prior, sums)
        mixed = gains + duals / RHO
        polynomial = jnp.einsum('jf,fcks->jcks', weights, mixed, precision=HIGHEST)
        prior = jnp.einsum('fj,jcks->fcks', basis, polynomial, precision=HIGHEST)
        duals = duals + RHO * (gains - prior)
    return (gains, duals, polynomial)
```

```python
from functools import partial

import jax
import jax.numpy as jnp
import numpy as np
from jax import lax
from jax.experimental import pallas as pl
from jax.experimental.pallas import tpu as pltpu
from jax.sharding import PartitionSpec as P

ITERS = 2
RHO = 16.0
LANES = 128
OUTER = 4


def split(block):
    return ([block[i] for i in range(4)], [block[i + 4] for i in range(4)])


def product(left, right):
    lr, li = left
    rr, ri = right
    out_real, out_imag = [], []
    for row in range(2):
        for col in range(2):
            a, b = 2 * row, 2 * row + 1
            out_real.append(lr[a] * rr[col] - li[a] * ri[col] + lr[b] * rr[col + 2] - li[b] * ri[col + 2])
            out_imag.append(lr[a] * ri[col] + li[a] * rr[col] + lr[b] * ri[col + 2] + li[b] * rr[col + 2])
    return (out_real, out_imag)


def product_right_adjoint(left, right):
    lr, li = left
    rr, ri = right
    out_real, out_imag = [], []
    for row in range(2):
        for col in range(2):
            a, b, c, d = 2 * row, 2 * row + 1, 2 * col, 2 * col + 1
            out_real.append(lr[a] * rr[c] + li[a] * ri[c] + lr[b] * rr[d] + li[b] * ri[d])
            out_imag.append(li[a] * rr[c] - lr[a] * ri[c] + li[b] * rr[d] - lr[b] * ri[d])
    return (out_real, out_imag)


def product_left_adjoint(left, right):
    lr, li = left
    rr, ri = right
    out_real, out_imag = [], []
    for row in range(2):
        for col in range(2):
            a, b, c, d = row, row + 2, col, col + 2
            out_real.append(lr[a] * rr[c] + li[a] * ri[c] + lr[b] * rr[d] + li[b] * ri[d])
            out_imag.append(lr[a] * ri[c] - li[a] * rr[c] + lr[b] * ri[d] - li[b] * rr[d])
    return (out_real, out_imag)


def normal(r, i, rows):
    (a, b), (c, d) = rows
    top = r[a] * r[a] + i[a] * i[a] + r[b] * r[b] + i[b] * i[b]
    bottom = r[c] * r[c] + i[c] * i[c] + r[d] * r[d] + i[d] * i[d]
    real = r[a] * r[c] + i[a] * i[c] + r[b] * r[d] + i[b] * i[d]
    imag = i[a] * r[c] - r[a] * i[c] + i[b] * r[d] - r[b] * i[d]
    return top, bottom, real, imag


def basis_weights(count):
    x = (2.0 * np.arange(count, dtype=np.float64) + 1.0) / count - 1.0
    basis = np.stack([np.ones_like(x), x, 1.5 * x * x - 0.5, 2.5 * x * x * x - 1.5 * x], axis=1)
    return np.linalg.solve(basis.T @ basis, basis.T)


def halves(value):
    high = value.astype(jnp.bfloat16)
    return high, (value - high.astype(jnp.float32)).astype(jnp.bfloat16)


def kernel(cfg, vis_ref, coh_ref, pairs_ref, gains_ref, duals_ref, poly_ref,
           gains_out, duals_out, poly_out,
           data, hot, terms, jones, mixed,
           tm_send, tm_recv, fq_send, fq_recv):
    F, K, S, nt, nf, inner, chunks, terms_poly = cfg
    CH = S // chunks
    FK = F * 8 * K
    tm = lax.axis_index("tm")
    fq = lax.axis_index("freq")
    z, y = tm // inner, tm % inner
    partner = fq + 1 - 2 * (fq % 2)

    def tm_at(dz, dy):
        return ((z + dz) % OUTER) * inner + (y + dy) % inner

    head = 8 + F * 8
    data[tm, 0:2, :] = pairs_ref[...].astype(jnp.float32)
    data[tm, 8:head, :] = vis_ref[...].reshape(F * 8, LANES)
    data[tm, head:, :] = coh_ref[...].astype(jnp.float32).reshape(F * 8 * K, LANES)

    barrier = pltpu.get_barrier_semaphore()
    peers = [{"tm": tm_at(d, 0)} for d in range(1, OUTER)]
    peers += [{"tm": tm_at(0, e)} for e in range(1, inner)]
    peers += [{"freq": partner}]
    peers += [{"freq": (fq + 2 * d) % nf} for d in range(1, nf // 2)]
    for peer in peers:
        pl.semaphore_signal(barrier, inc=1, device_id=peer, device_id_type=pl.DeviceIdType.MESH)

    def load_gains(gains):
        high, low = halves(gains)
        jones[0:FK, :] = high
        jones[FK : 2 * FK, :] = low

    load_gains(gains_ref[...].reshape(FK, S))
    pl.semaphore_wait(barrier, len(peers))

    def tm_copy(block, slot, device):
        return pltpu.make_async_remote_copy(
            src_ref=data.at[block], dst_ref=data.at[block],
            send_sem=tm_send.at[slot], recv_sem=tm_recv.at[block],
            device_id={"tm": device}, device_id_type=pl.DeviceIdType.MESH)

    sends = []

    def send(block, device):
        copy = tm_copy(block, len(sends), device)
        copy.start()
        sends.append(copy)

    for e in range(1, inner):
        send(tm, tm_at(0, e))
    for d in (1, 3, 2):
        send(tm, tm_at(d, 0))

    stations = lax.broadcasted_iota(jnp.int32, (S, LANES), 0).astype(jnp.float32)

    def columns(block, half):
        return pl.ds(pl.multiple_of(block * 2 * LANES + half * LANES, LANES), LANES)

    def make_hot(block):
        for half in range(2):
            row = data[block, half : half + 1, :]
            hot[:, columns(block, half)] = jnp.where(stations == row, 1.0, 0.0).astype(jnp.bfloat16)

    def rows_sums(block):
        both = pl.ds(pl.multiple_of(block * 2 * LANES, 2 * LANES), 2 * LANES)
        taken = jnp.dot(jones[...], hot[:, both], preferred_element_type=jnp.float32)
        taken = taken[:FK] + taken[FK:]
        for f in range(F):
            base = f * 8 * K
            first = split([taken[base + c * K : base + (c + 1) * K, :LANES] for c in range(8)])
            second = split([taken[base + c * K : base + (c + 1) * K, LANES:] for c in range(8)])
            start = head + base
            sky = split([data[block, start + c * K : start + (c + 1) * K, :] for c in range(8)])
            left = product(first, sky)
            right = product_right_adjoint(sky, second)
            model = product_right_adjoint(left, second)
            model = model[0] + model[1]
            residual = []
            for c in range(8):
                seen = data[block, 8 + f * 8 + c : 8 + f * 8 + c + 1, :]
                residual.append(jnp.broadcast_to(seen - jnp.sum(model[c], axis=0, keepdims=True), (K, LANES)))
            residual = split(residual)
            ends = []
            out = product_right_adjoint(residual, right)
            ends.append(out[0] + out[1] + list(normal(right[0], right[1], ((0, 1), (2, 3)))))
            out = product_left_adjoint(residual, left)
            top, bottom, real, imag = normal(left[0], left[1], ((0, 2), (1, 3)))
            ends.append(out[0] + out[1] + [top, bottom, real, -imag])
            for half in range(2):
                high, low = halves(jnp.concatenate(ends[half], axis=0))
                terms[f * 12 * K : (f + 1) * 12 * K, columns(block, half)] = high
                terms[(F + f) * 12 * K : (F + f + 1) * 12 * K, columns(block, half)] = low

    def basis_at(f):
        channel = (fq * F + f).astype(jnp.float32)
        x = (2.0 * channel + 1.0) / (F * nf) - 1.0
        return [None, x, 1.5 * x * x - 0.5, 2.5 * x * x * x - 1.5 * x]

    bases = [basis_at(f) for f in range(F)]

    def from_basis(f, coefficients):
        total = coefficients[0]
        for j in range(1, terms_poly):
            total = total + bases[f][j] * coefficients[j]
        return total

    def update(source, damping, chunk):
        lanes = slice(chunk * CH, (chunk + 1) * CH)
        sums = lax.dot_general(terms[...], hot[lanes, :], (((1,), (1,)), ((), ())),
                               preferred_element_type=jnp.float32)
        half = F * 12 * K
        sums = sums[:half] + sums[half:]
        for f in range(F):
            part = [sums[(f * 12 + c) * K : (f * 12 + c + 1) * K] for c in range(12)]
            old, step = [], []
            for c in range(8):
                prior = from_basis(f, [poly_ref[j, c, :, lanes] for j in range(terms_poly)])
                gain = source[f, c, :, lanes]
                old.append(gain)
                step.append(part[c] - duals_ref[f, c, :, lanes] - RHO * (gain - prior))
            top, bottom, real, imag = part[8:]
            shift = damping * 0.5 * (top + bottom) + RHO
            upper, lower = top + shift, bottom + shift
            scale = 1.0 / (upper * lower - real * real - imag * imag)
            a, d, br, bi = lower * scale, upper * scale, -real * scale, -imag * scale
            sr, si = split(step)
            for row in range(2):
                p, q = 2 * row, 2 * row + 1
                gains_out[f, p, :, lanes] = old[p] + sr[p] * a + sr[q] * br + si[q] * bi
                gains_out[f, p + 4, :, lanes] = old[p + 4] + si[p] * a + si[q] * br - sr[q] * bi
                gains_out[f, q, :, lanes] = old[q] + sr[p] * br - si[p] * bi + sr[q] * d
                gains_out[f, q + 4, :, lanes] = old[q + 4] + si[p] * br + sr[p] * bi + si[q] * d

    def arrived(block):
        tm_copy(block, 0, tm).wait_recv()

    make_hot(tm)
    rows_sums(tm)
    for dz in (0, 1, 3, 2):
        if dz:
            block = tm_at(dz, 0)
            arrived(block)
            for e in range(1, inner):
                send(block, tm_at(0, e))
            make_hot(block)
            rows_sums(block)
    for dz in (0, 1, 3, 2):
        for e in range(1, inner):
            block = tm_at(dz, e)
            arrived(block)
            make_hot(block)
            rows_sums(block)

    for chunk in range(chunks):
        update(gains_ref, 12.0, chunk)
    for inner_step in range(1, ITERS):
        load_gains(gains_out[...].reshape(FK, S))

        @pl.loop(0, nt)
        def _(block):
            rows_sums(block)

        if inner_step < ITERS - 1:
            for chunk in range(chunks):
                update(gains_out, 12.0 * 0.5**inner_step, chunk)

    def fq_copy(owner, chunk, slot, device):
        return pltpu.make_async_remote_copy(
            src_ref=mixed.at[owner, chunk], dst_ref=mixed.at[owner, chunk],
            send_sem=fq_send.at[slot, chunk], recv_sem=fq_recv.at[owner, chunk],
            device_id={"freq": device}, device_id_type=pl.DeviceIdType.MESH)

    fq_sends = []

    def fq_start(owner, chunk, slot, device):
        copy = fq_copy(owner, chunk, slot, device)
        copy.start()
        fq_sends.append(copy)

    def fq_push(chunk):
        for d in range(1, nf // 2):
            fq_start(fq, chunk, d, (fq + 2 * d) % nf)
        fq_start(fq, chunk, 0, partner)

    for chunk in range(chunks):
        lanes = slice(chunk * CH, (chunk + 1) * CH)
        update(gains_out, 12.0 * 0.5 ** (ITERS - 1), chunk)
        value = gains_out[:, :, :, lanes] + duals_ref[:, :, :, lanes] * (1.0 / RHO)
        mixed[fq, chunk] = value.reshape(FK, CH)
        fq_push(chunk)

    weights = basis_weights(F * nf)
    for chunk in range(chunks):
        for d in range(1, nf // 2):
            owner = (fq - 2 * d + nf) % nf
            fq_copy(owner, chunk, 0, partner).wait_recv()
            fq_start(owner, chunk, nf // 2 + d, partner)
    for chunk in range(chunks):
        lanes = slice(chunk * CH, (chunk + 1) * CH)
        fq_copy(partner, chunk, 0, partner).wait_recv()
        for d in range(1, nf // 2):
            owner = (partner - 2 * d + nf) % nf
            fq_copy(owner, chunk, 0, partner).wait_recv()
        for c in range(8):
            rows = [mixed[n // F, chunk, ((n % F) * 8 + c) * K : ((n % F) * 8 + c + 1) * K, :] for n in range(nf * F)]
            coefficients = []
            for j in range(terms_poly):
                total = float(weights[j, 0]) * rows[0]
                for n in range(1, nf * F):
                    total = total + float(weights[j, n]) * rows[n]
                poly_out[j, c, :, lanes] = total
                coefficients.append(total)
            for f in range(F):
                prior = from_basis(f, coefficients)
                duals_out[f, c, :, lanes] = duals_ref[f, c, :, lanes] + RHO * (gains_out[f, c, :, lanes] - prior)
    for copy in sends + fq_sends:
        copy.wait_send()


def solution(mesh):
    nt, nf = mesh.shape["tm"], mesh.shape["freq"]

    def shards(visibilities, coherencies, pairs, gains_start, duals_start, poly_start):
        F, _, K, S = gains_start.shape
        inner = nt // OUTER
        chunks = 2
        FK = F * 8 * K
        cfg = (F, K, S, nt, nf, inner, chunks, poly_start.shape[0])
        like = lambda x: jax.ShapeDtypeStruct(x.shape, jnp.float32)
        vmem = pl.BlockSpec(memory_space=pltpu.VMEM)
        return pl.pallas_call(
            partial(kernel, cfg),
            out_shape=(like(gains_start), like(duals_start), like(poly_start)),
            in_specs=[vmem] * 6,
            out_specs=(vmem,) * 3,
            scratch_shapes=[
                pltpu.VMEM((nt, 8 + F * 8 + F * 8 * K, LANES), jnp.float32),
                pltpu.VMEM((S, nt * 2 * LANES), jnp.bfloat16),
                pltpu.VMEM((2 * F * 12 * K, nt * 2 * LANES), jnp.bfloat16),
                pltpu.VMEM((2 * FK, S), jnp.bfloat16),
                pltpu.VMEM((nf, chunks, FK, S // chunks), jnp.float32),
                pltpu.SemaphoreType.DMA((nt,)),
                pltpu.SemaphoreType.DMA((nt,)),
                pltpu.SemaphoreType.DMA((nf + 1, chunks)),
                pltpu.SemaphoreType.DMA((nf, chunks)),
            ],
            compiler_params=pltpu.CompilerParams(collective_id=0, has_side_effects=True,
                                                 vmem_limit_bytes=60 * 2**20),
        )(visibilities, coherencies, pairs, gains_start, duals_start, poly_start)

    placed = (
        P("freq", None, "tm"),
        P("freq", None, None, "tm"),
        P(None, "tm"),
        P("freq", None, None, None),
        P("freq", None, None, None),
        P(),
    )
    return jax.shard_map(
        shards,
        mesh=mesh,
        in_specs=placed,
        out_specs=(P("freq", None, None, None), P("freq", None, None, None), P()),
        check_vma=False,
    )
```

```python
from functools import partial

import jax
import jax.numpy as jnp
import numpy as np
from jax import lax
from jax.experimental import pallas as pl
from jax.experimental.pallas import tpu as pltpu
from jax.sharding import PartitionSpec as P

ITERS = 2
RHO = 16.0
LANES = 128
OUTER = 4


def split(block):
    return ([block[i] for i in range(4)], [block[i + 4] for i in range(4)])


def product(left, right):
    lr, li = left
    rr, ri = right
    out_real, out_imag = [], []
    for row in range(2):
        for col in range(2):
            a, b = 2 * row, 2 * row + 1
            out_real.append(lr[a] * rr[col] - li[a] * ri[col] + lr[b] * rr[col + 2] - li[b] * ri[col + 2])
            out_imag.append(lr[a] * ri[col] + li[a] * rr[col] + lr[b] * ri[col + 2] + li[b] * rr[col + 2])
    return (out_real, out_imag)


def product_right_adjoint(left, right):
    lr, li = left
    rr, ri = right
    out_real, out_imag = [], []
    for row in range(2):
        for col in range(2):
            a, b, c, d = 2 * row, 2 * row + 1, 2 * col, 2 * col + 1
            out_real.append(lr[a] * rr[c] + li[a] * ri[c] + lr[b] * rr[d] + li[b] * ri[d])
            out_imag.append(li[a] * rr[c] - lr[a] * ri[c] + li[b] * rr[d] - lr[b] * ri[d])
    return (out_real, out_imag)


def product_left_adjoint(left, right):
    lr, li = left
    rr, ri = right
    out_real, out_imag = [], []
    for row in range(2):
        for col in range(2):
            a, b, c, d = row, row + 2, col, col + 2
            out_real.append(lr[a] * rr[c] + li[a] * ri[c] + lr[b] * rr[d] + li[b] * ri[d])
            out_imag.append(lr[a] * ri[c] - li[a] * rr[c] + lr[b] * ri[d] - li[b] * rr[d])
    return (out_real, out_imag)


def normal(r, i, rows):
    (a, b), (c, d) = rows
    top = r[a] * r[a] + i[a] * i[a] + r[b] * r[b] + i[b] * i[b]
    bottom = r[c] * r[c] + i[c] * i[c] + r[d] * r[d] + i[d] * i[d]
    real = r[a] * r[c] + i[a] * i[c] + r[b] * r[d] + i[b] * i[d]
    imag = i[a] * r[c] - r[a] * i[c] + i[b] * r[d] - r[b] * i[d]
    return top, bottom, real, imag


def basis_weights(count):
    x = (2.0 * np.arange(count, dtype=np.float64) + 1.0) / count - 1.0
    basis = np.stack([np.ones_like(x), x, 1.5 * x * x - 0.5, 2.5 * x * x * x - 1.5 * x], axis=1)
    return np.linalg.solve(basis.T @ basis, basis.T)


def halves(value):
    high = value.astype(jnp.bfloat16)
    return high, (value - high.astype(jnp.float32)).astype(jnp.bfloat16)


def from_basis(bases, f, coefficients):
    total = coefficients[0]
    for j in range(1, len(coefficients)):
        total = total + bases[f][j] * coefficients[j]
    return total


def local_bases(F, nf):
    bases = []
    for f in range(F):
        channel = (lax.axis_index("freq") * F + f).astype(jnp.float32)
        x = (2.0 * channel + 1.0) / (F * nf) - 1.0
        bases.append([None, x, 1.5 * x * x - 0.5, 2.5 * x * x * x - 1.5 * x])
    return bases


def fit_kernel(cfg, mixed, gains_ref, duals_ref, gains_out, duals_out, poly_out):
    F, K, S, nt, nf, inner, chunks, terms_poly = cfg
    CH = S // chunks
    FK = F * 8 * K
    weights = basis_weights(F * nf)
    bases = local_bases(F, nf)
    gains_out[...] = gains_ref[...]

    def rows(n, chunk, c):
        at = ((n % F) * 8 + c) * K
        return mixed[n // F, chunk, at // (FK // 2), at % (FK // 2) : at % (FK // 2) + K, :]

    for chunk in range(mixed.shape[1]):
        lanes = slice(chunk * CH, (chunk + 1) * CH)
        for c in range(8):
            values = [rows(n, chunk, c) for n in range(nf * F)]
            coefficients = []
            for j in range(terms_poly):
                total = float(weights[j, 0]) * values[0]
                for n in range(1, nf * F):
                    total = total + float(weights[j, n]) * values[n]
                poly_out[j, c, :, lanes] = total
                coefficients.append(total)
            for f in range(F):
                prior = from_basis(bases, f, coefficients)
                duals_out[f, c, :, lanes] = duals_ref[f, c, :, lanes] + RHO * (gains_ref[f, c, :, lanes] - prior)


def kernel(cfg, vis_hbm, coh_hbm, pairs_hbm, gains_hbm, duals_hbm, poly_hbm,
           gains_out, mixed,
           data, hot, terms, jones, taken, vis_ref, coh_ref, pairs_ref, gains_ref, duals_ref, poly_ref,
           tm_send, tm_recv, fq_send, fq_recv, load_sem):
    F, K, S, nt, nf, inner, chunks, terms_poly = cfg
    CH = S // chunks
    FK = F * 8 * K
    tm = lax.axis_index("tm")
    fq = lax.axis_index("freq")
    z, y = tm // inner, tm % inner
    partner = fq + 1 - 2 * (fq % 2)
    mate = tm + 1 - 2 * (tm % 2)
    MESH = pl.DeviceIdType.MESH

    loads = [pltpu.make_async_copy(src, dst, load_sem.at[i]) for i, (src, dst) in enumerate(
        ((gains_hbm, gains_ref), (duals_hbm, duals_ref), (poly_hbm, poly_ref),
         (coh_hbm, coh_ref), (vis_hbm, vis_ref), (pairs_hbm, pairs_ref)))]

    def tm_at(dz, dy):
        return ((z + dz) % OUTER) * inner + (y + dy) % inner

    for load in reversed(loads):
        load.start()
    barrier = pltpu.get_barrier_semaphore()

    def greet(peer):
        pl.semaphore_signal(barrier, inc=1, device_id=peer, device_id_type=MESH)

    peers = [{"tm": tm_at(d, 0)} for d in range(1, OUTER)]
    peers += [{"tm": tm_at(0, e)} for e in range(1, inner)]
    peers += [{"freq": partner}]
    peers += [{"freq": (fq + 2 * d) % nf} for d in range(1, nf // 2)]
    for peer in peers:
        greet(peer)
    for load in loads[3:]:
        load.wait()
    data[tm, 0, 0:2, :] = pairs_ref[...].astype(jnp.float32)
    for f in range(F):
        data[tm, f, 8:16, :] = vis_ref[f]
        data[tm, f, 16:, :] = coh_ref[f].astype(jnp.float32).reshape(8 * K, LANES)

    def load_gains(gains):
        high, low = halves(gains)
        jones[0:FK, :] = high
        jones[FK : 2 * FK, :] = low

    pl.semaphore_wait(barrier, len(peers))

    def tm_copy(block, f, slot, device):
        rows = pl.ds(0, 16 + 8 * K) if f == 0 else pl.ds(8, 8 + 8 * K)
        return pltpu.make_async_remote_copy(
            src_ref=data.at[block, f, rows], dst_ref=data.at[block, f, rows],
            send_sem=tm_send.at[slot, f], recv_sem=tm_recv.at[block, f],
            device_id={"tm": device}, device_id_type=MESH)

    def arrived(block, f):
        tm_copy(block, f, 0, mate).wait_recv()

    sends = []

    def send(block, f, slot, device):
        copy = tm_copy(block, f, slot, device)
        copy.start()
        sends.append(copy)

    def relay(d, f):
        for e in range(1, inner):
            send(tm_at(d, 0), f, OUTER + d * inner + e, tm_at(0, e))

    for f in range(F):
        for d in (1, 3, 2):
            send(tm, f, d, tm_at(d, 0))
        relay(0, f)

    stations = lax.broadcasted_iota(jnp.int32, (S, LANES), 0).astype(jnp.float32)

    def columns(block, half):
        return pl.ds(pl.multiple_of(block * 2 * LANES + half * LANES, LANES), LANES)

    def make_hot(block):
        for half in range(2):
            row = data[block, 0, half : half + 1, :]
            hot[:, columns(block, half)] = jnp.where(stations == row, 1.0, 0.0).astype(jnp.bfloat16)

    def gather(block):
        both = pl.ds(pl.multiple_of(block * 2 * LANES, 2 * LANES), 2 * LANES)
        found = jnp.dot(jones[...], hot[:, both], preferred_element_type=jnp.float32)
        taken[block] = found[:FK] + found[FK:]

    def rows_sums(block, channels):
        for f in channels:
            base = f * 8 * K
            first = split([taken[block, base + c * K : base + (c + 1) * K, :LANES] for c in range(8)])
            second = split([taken[block, base + c * K : base + (c + 1) * K, LANES:] for c in range(8)])
            sky = split([data[block, f, 16 + c * K : 16 + (c + 1) * K, :] for c in range(8)])
            left = product(first, sky)
            right = product_right_adjoint(sky, second)
            model = product_right_adjoint(left, second)
            model = model[0] + model[1]
            residual = []
            for c in range(8):
                seen = data[block, f, 8 + c : 9 + c, :]
                residual.append(jnp.broadcast_to(seen - jnp.sum(model[c], axis=0, keepdims=True), (K, LANES)))
            residual = split(residual)
            ends = []
            out = product_right_adjoint(residual, right)
            ends.append(out[0] + out[1] + list(normal(right[0], right[1], ((0, 1), (2, 3)))))
            out = product_left_adjoint(residual, left)
            top, bottom, real, imag = normal(left[0], left[1], ((0, 2), (1, 3)))
            ends.append(out[0] + out[1] + [top, bottom, real, -imag])
            for half in range(2):
                high, low = halves(jnp.concatenate(ends[half], axis=0))
                terms[f * 12 * K : (f + 1) * 12 * K, columns(block, half)] = high
                terms[(F + f) * 12 * K : (F + f + 1) * 12 * K, columns(block, half)] = low

    bases = local_bases(F, nf)

    def update(source, damping, chunk):
        lanes = slice(chunk * CH, (chunk + 1) * CH)
        sums = lax.dot_general(terms[...], hot[lanes, :], (((1,), (1,)), ((), ())),
                               preferred_element_type=jnp.float32)
        half = F * 12 * K
        sums = sums[:half] + sums[half:]
        for f in range(F):
            part = [sums[(f * 12 + c) * K : (f * 12 + c + 1) * K] for c in range(12)]
            old, step = [], []
            for c in range(8):
                prior = from_basis(bases, f, [poly_ref[j, c, :, lanes] for j in range(terms_poly)])
                gain = source[f, c, :, lanes]
                old.append(gain)
                step.append(part[c] - duals_ref[f, c, :, lanes] - RHO * (gain - prior))
            top, bottom, real, imag = part[8:]
            shift = damping * 0.5 * (top + bottom) + RHO
            upper, lower = top + shift, bottom + shift
            scale = 1.0 / (upper * lower - real * real - imag * imag)
            a, d, br, bi = lower * scale, upper * scale, -real * scale, -imag * scale
            sr, si = split(step)
            for row in range(2):
                p, q = 2 * row, 2 * row + 1
                gains_out[f, p, :, lanes] = old[p] + sr[p] * a + sr[q] * br + si[q] * bi
                gains_out[f, p + 4, :, lanes] = old[p + 4] + si[p] * a + si[q] * br - sr[q] * bi
                gains_out[f, q, :, lanes] = old[q] + sr[p] * br - si[p] * bi + sr[q] * d
                gains_out[f, q + 4, :, lanes] = old[q + 4] + si[p] * br + sr[p] * bi + si[q] * d

    def take(block, f):
        if f == 0:
            make_hot(block)
            gather(block)
        rows_sums(block, [f])

    loads[0].wait()
    load_gains(gains_ref[...].reshape(FK, S))
    for f in range(F):
        take(tm, f)
    for f in range(F):
        for d in (1, 3):
            arrived(tm_at(d, 0), f)
            relay(d, f)
    for e in range(1, inner):
        for f in range(F):
            arrived(tm_at(0, e), f)
            take(tm_at(0, e), f)
    for f in range(F):
        arrived(tm_at(2, 0), f)
        relay(2, f)
    for d in (1, 3, 2):
        for f in range(F):
            take(tm_at(d, 0), f)
    for d in (1, 3, 2):
        for e in range(1, inner):
            for f in range(F):
                arrived(tm_at(d, e), f)
                take(tm_at(d, e), f)

    loads[1].wait()
    loads[2].wait()
    for chunk in range(chunks):
        update(gains_ref, 12.0, chunk)
    for inner_step in range(1, ITERS):
        load_gains(gains_out[...].reshape(FK, S))

        @pl.loop(0, nt)
        def _(block):
            gather(block)
            rows_sums(block, range(F))

        if inner_step < ITERS - 1:
            for chunk in range(chunks):
                update(gains_out, 12.0 * 0.5**inner_step, chunk)

    def fq_copy(owner, chunk, slot, device):
        return pltpu.make_async_remote_copy(
            src_ref=mixed.at[owner, chunk], dst_ref=mixed.at[owner, chunk],
            send_sem=fq_send.at[slot, chunk], recv_sem=fq_recv.at[owner, chunk],
            device_id={"freq": device}, device_id_type=MESH)

    fq_sends = []

    def fq_start(owner, chunk, slot, device):
        copy = fq_copy(owner, chunk, slot, device)
        copy.start()
        fq_sends.append(copy)

    others = nf // 2
    for chunk in range(chunks):
        lanes = slice(chunk * CH, (chunk + 1) * CH)
        update(gains_out, 12.0 * 0.5 ** (ITERS - 1), chunk)
        value = gains_out[:, :, :, lanes] + duals_ref[:, :, :, lanes] * (1.0 / RHO)
        mixed[fq, chunk] = value.reshape(2, FK // 2, CH)
        for d in range(1, others):
            fq_start(fq, chunk, d, (fq + 2 * d) % nf)
        fq_start(fq, chunk, 0, partner)

    for chunk in range(chunks):
        for d in range(1, others):
            owner = (fq - 2 * d + nf) % nf
            fq_copy(owner, chunk, 0, partner).wait_recv()
            fq_start(owner, chunk, others + d, partner)
    for chunk in range(chunks):
        fq_copy(partner, chunk, 0, partner).wait_recv()
        for d in range(1, others):
            fq_copy((partner - 2 * d + nf) % nf, chunk, 0, partner).wait_recv()
    for copy in sends + fq_sends:
        copy.wait_send()


def solution(mesh):
    nt, nf = mesh.shape["tm"], mesh.shape["freq"]

    def shards(visibilities, coherencies, pairs, gains_start, duals_start, poly_start):
        F, _, K, S = gains_start.shape
        inner = nt // OUTER
        chunks = 2
        FK = F * 8 * K
        CH = S // chunks
        cfg = (F, K, S, nt, nf, inner, chunks, poly_start.shape[0])
        like = lambda x: jax.ShapeDtypeStruct(x.shape, jnp.float32)
        vmem = pl.BlockSpec(memory_space=pltpu.VMEM)
        hbm = pl.BlockSpec(memory_space=pltpu.HBM)
        gains, mixed = pl.pallas_call(
            partial(kernel, cfg),
            out_shape=(like(gains_start), jax.ShapeDtypeStruct((nf, chunks, 2, FK // 2, CH), jnp.float32)),
            in_specs=[hbm] * 6,
            out_specs=(vmem,) * 2,
            scratch_shapes=[
                pltpu.VMEM((nt, F, 16 + 8 * K, LANES), jnp.float32),
                pltpu.VMEM((S, nt * 2 * LANES), jnp.bfloat16),
                pltpu.VMEM((2 * F * 12 * K, nt * 2 * LANES), jnp.bfloat16),
                pltpu.VMEM((2 * FK, S), jnp.bfloat16),
                pltpu.VMEM((nt, FK, 2 * LANES), jnp.float32),
                pltpu.VMEM(visibilities.shape, jnp.float32),
                pltpu.VMEM(coherencies.shape, jnp.bfloat16),
                pltpu.VMEM(pairs.shape, jnp.int32),
                pltpu.VMEM(gains_start.shape, jnp.float32),
                pltpu.VMEM(gains_start.shape, jnp.float32),
                pltpu.VMEM(poly_start.shape, jnp.float32),
                pltpu.SemaphoreType.DMA((OUTER + OUTER * inner, F)),
                pltpu.SemaphoreType.DMA((nt, F)),
                pltpu.SemaphoreType.DMA((nf + 1, chunks)),
                pltpu.SemaphoreType.DMA((nf, chunks)),
                pltpu.SemaphoreType.DMA((6,)),
            ],
            compiler_params=pltpu.CompilerParams(collective_id=0, has_side_effects=True,
                                                 vmem_limit_bytes=58 * 2**20),
        )(visibilities, coherencies, pairs, gains_start, duals_start, poly_start)
        own = pl.BlockSpec((F, 8, K, CH), lambda i: (0, 0, 0, i))
        return pl.pallas_call(
            partial(fit_kernel, cfg),
            grid=(chunks,),
            out_shape=(like(gains_start), like(duals_start), like(poly_start)),
            in_specs=[pl.BlockSpec((nf, 1, 2, FK // 2, CH), lambda i: (0, i, 0, 0, 0)), own, own],
            out_specs=(own, own, pl.BlockSpec((poly_start.shape[0], 8, K, CH), lambda i: (0, 0, 0, i))),
            compiler_params=pltpu.CompilerParams(vmem_limit_bytes=60 * 2**20),
        )(mixed, gains, duals_start)

    placed = (
        P("freq", None, "tm"),
        P("freq", None, None, "tm"),
        P(None, "tm"),
        P("freq", None, None, None),
        P("freq", None, None, None),
        P(),
    )
    return jax.shard_map(
        shards,
        mesh=mesh,
        in_specs=placed,
        out_specs=(P("freq", None, None, None), P("freq", None, None, None), P()),
        check_vma=False,
    )
```

```python
from functools import partial

import jax
import jax.numpy as jnp
import numpy as np
from jax import lax
from jax.experimental import pallas as pl
from jax.experimental.pallas import tpu as pltpu
from jax.sharding import PartitionSpec as P

ITERS = 2
RHO = 16.0
LANES = 128
OUTER = 4


def split(block):
    return ([block[i] for i in range(4)], [block[i + 4] for i in range(4)])


def product(left, right):
    lr, li = left
    rr, ri = right
    out_real, out_imag = [], []
    for row in range(2):
        for col in range(2):
            a, b = 2 * row, 2 * row + 1
            out_real.append(lr[a] * rr[col] - li[a] * ri[col] + lr[b] * rr[col + 2] - li[b] * ri[col + 2])
            out_imag.append(lr[a] * ri[col] + li[a] * rr[col] + lr[b] * ri[col + 2] + li[b] * rr[col + 2])
    return (out_real, out_imag)


def product_right_adjoint(left, right):
    lr, li = left
    rr, ri = right
    out_real, out_imag = [], []
    for row in range(2):
        for col in range(2):
            a, b, c, d = 2 * row, 2 * row + 1, 2 * col, 2 * col + 1
            out_real.append(lr[a] * rr[c] + li[a] * ri[c] + lr[b] * rr[d] + li[b] * ri[d])
            out_imag.append(li[a] * rr[c] - lr[a] * ri[c] + li[b] * rr[d] - lr[b] * ri[d])
    return (out_real, out_imag)


def product_left_adjoint(left, right):
    lr, li = left
    rr, ri = right
    out_real, out_imag = [], []
    for row in range(2):
        for col in range(2):
            a, b, c, d = row, row + 2, col, col + 2
            out_real.append(lr[a] * rr[c] + li[a] * ri[c] + lr[b] * rr[d] + li[b] * ri[d])
            out_imag.append(lr[a] * ri[c] - li[a] * rr[c] + lr[b] * ri[d] - li[b] * rr[d])
    return (out_real, out_imag)


def normal(r, i, rows):
    (a, b), (c, d) = rows
    top = r[a] * r[a] + i[a] * i[a] + r[b] * r[b] + i[b] * i[b]
    bottom = r[c] * r[c] + i[c] * i[c] + r[d] * r[d] + i[d] * i[d]
    real = r[a] * r[c] + i[a] * i[c] + r[b] * r[d] + i[b] * i[d]
    imag = i[a] * r[c] - r[a] * i[c] + i[b] * r[d] - r[b] * i[d]
    return top, bottom, real, imag


def basis_weights(count):
    x = (2.0 * np.arange(count, dtype=np.float64) + 1.0) / count - 1.0
    basis = np.stack([np.ones_like(x), x, 1.5 * x * x - 0.5, 2.5 * x * x * x - 1.5 * x], axis=1)
    return np.linalg.solve(basis.T @ basis, basis.T)


def halves(value):
    high = value.astype(jnp.bfloat16)
    return high, (value - high.astype(jnp.float32)).astype(jnp.bfloat16)


def from_basis(bases, f, coefficients):
    total = coefficients[0]
    for j in range(1, len(coefficients)):
        total = total + bases[f][j] * coefficients[j]
    return total


def local_bases(F, nf):
    bases = []
    for f in range(F):
        channel = (lax.axis_index("freq") * F + f).astype(jnp.float32)
        x = (2.0 * channel + 1.0) / (F * nf) - 1.0
        bases.append([None, x, 1.5 * x * x - 0.5, 2.5 * x * x * x - 1.5 * x])
    return bases


def fit_kernel(cfg, mixed, gains_ref, duals_ref, gains_out, duals_out, poly_out):
    F, K, S, nt, nf, inner, chunks, terms_poly = cfg
    CH = S // chunks
    FK = F * 8 * K
    weights = basis_weights(F * nf)
    bases = local_bases(F, nf)
    gains_out[...] = gains_ref[...]

    def rows(n, chunk, c):
        at = ((n % F) * 8 + c) * K
        return mixed[n // F, chunk, at // (FK // 2), at % (FK // 2) : at % (FK // 2) + K, :]

    for chunk in range(mixed.shape[1]):
        lanes = slice(chunk * CH, (chunk + 1) * CH)
        for c in range(8):
            values = [rows(n, chunk, c) for n in range(nf * F)]
            coefficients = []
            for j in range(terms_poly):
                total = float(weights[j, 0]) * values[0]
                for n in range(1, nf * F):
                    total = total + float(weights[j, n]) * values[n]
                poly_out[j, c, :, lanes] = total
                coefficients.append(total)
            for f in range(F):
                prior = from_basis(bases, f, coefficients)
                duals_out[f, c, :, lanes] = duals_ref[f, c, :, lanes] + RHO * (gains_ref[f, c, :, lanes] - prior)


def kernel(cfg, vis_hbm, coh_hbm, pairs_hbm, gains_hbm, duals_hbm, poly_hbm,
           gains_out, mixed,
           data, hot, terms, jones, taken, vis_ref, coh_ref, pairs_ref, gains_ref, duals_ref, poly_ref,
           tm_send, tm_recv, fq_send, fq_recv, load_sem):
    F, K, S, nt, nf, inner, chunks, terms_poly = cfg
    CH = S // chunks
    FK = F * 8 * K
    tm = lax.axis_index("tm")
    fq = lax.axis_index("freq")
    z, y = tm // inner, tm % inner
    partner = fq + 1 - 2 * (fq % 2)
    mate = tm + 1 - 2 * (tm % 2)
    MESH = pl.DeviceIdType.MESH

    loads = [pltpu.make_async_copy(src, dst, load_sem.at[i]) for i, (src, dst) in enumerate(
        ((gains_hbm, gains_ref), (duals_hbm, duals_ref), (poly_hbm, poly_ref),
         (coh_hbm, coh_ref), (vis_hbm, vis_ref), (pairs_hbm, pairs_ref)))]

    def tm_at(dz, dy):
        return ((z + dz) % OUTER) * inner + (y + dy) % inner

    for load in reversed(loads):
        load.start()
    barrier = pltpu.get_barrier_semaphore()

    def greet(peer):
        pl.semaphore_signal(barrier, inc=1, device_id=peer, device_id_type=MESH)

    peers = [{"tm": tm_at(d, 0)} for d in range(1, OUTER)]
    peers += [{"tm": tm_at(0, e)} for e in range(1, inner)]
    peers += [{"freq": partner}]
    peers += [{"freq": (fq + 2 * d) % nf} for d in range(1, nf // 2)]
    for peer in peers:
        greet(peer)
    for load in loads[3:]:
        load.wait()
    data[tm, 0, 0:2, :] = pairs_ref[...].astype(jnp.float32)
    for f in range(F):
        data[tm, f, 8:16, :] = vis_ref[f]
        data[tm, f, 16:, :] = coh_ref[f].astype(jnp.float32).reshape(8 * K, LANES)

    def load_gains(gains):
        high, low = halves(gains)
        jones[0:FK, :] = high
        jones[FK : 2 * FK, :] = low

    pl.semaphore_wait(barrier, len(peers))

    def tm_copy(block, f, slot, device):
        rows = pl.ds(0, 16 + 8 * K) if f == 0 else pl.ds(8, 8 + 8 * K)
        return pltpu.make_async_remote_copy(
            src_ref=data.at[block, f, rows], dst_ref=data.at[block, f, rows],
            send_sem=tm_send.at[slot, f], recv_sem=tm_recv.at[block, f],
            device_id={"tm": device}, device_id_type=MESH)

    def arrived(block, f):
        tm_copy(block, f, 0, mate).wait_recv()

    sends = []

    def send(block, f, slot, device):
        copy = tm_copy(block, f, slot, device)
        copy.start()
        sends.append(copy)

    def relay(d, f):
        for e in range(1, inner):
            send(tm_at(d, 0), f, OUTER + d * inner + e, tm_at(0, e))

    for f in range(F):
        for d in (1, 3, 2):
            send(tm, f, d, tm_at(d, 0))
        relay(0, f)

    stations = lax.broadcasted_iota(jnp.int32, (S, LANES), 0).astype(jnp.float32)

    def columns(block, half):
        return pl.ds(pl.multiple_of(block * 2 * LANES + half * LANES, LANES), LANES)

    def make_hot(block):
        for half in range(2):
            row = data[block, 0, half : half + 1, :]
            hot[:, columns(block, half)] = jnp.where(stations == row, 1.0, 0.0).astype(jnp.bfloat16)

    def gather(block):
        both = pl.ds(pl.multiple_of(block * 2 * LANES, 2 * LANES), 2 * LANES)
        found = jnp.dot(jones[...], hot[:, both], preferred_element_type=jnp.float32)
        taken[block] = found[:FK] + found[FK:]

    def rows_sums(block, channels):
        for f in channels:
            base = f * 8 * K
            first = split([taken[block, base + c * K : base + (c + 1) * K, :LANES] for c in range(8)])
            second = split([taken[block, base + c * K : base + (c + 1) * K, LANES:] for c in range(8)])
            sky = split([data[block, f, 16 + c * K : 16 + (c + 1) * K, :] for c in range(8)])
            left = product(first, sky)
            right = product_right_adjoint(sky, second)
            model = product_right_adjoint(left, second)
            model = model[0] + model[1]
            residual = []
            for c in range(8):
                seen = data[block, f, 8 + c : 9 + c, :]
                residual.append(jnp.broadcast_to(seen - jnp.sum(model[c], axis=0, keepdims=True), (K, LANES)))
            residual = split(residual)
            ends = []
            out = product_right_adjoint(residual, right)
            ends.append(out[0] + out[1] + list(normal(right[0], right[1], ((0, 1), (2, 3)))))
            out = product_left_adjoint(residual, left)
            top, bottom, real, imag = normal(left[0], left[1], ((0, 2), (1, 3)))
            ends.append(out[0] + out[1] + [top, bottom, real, -imag])
            for half in range(2):
                high, low = halves(jnp.concatenate(ends[half], axis=0))
                terms[f * 12 * K : (f + 1) * 12 * K, columns(block, half)] = high
                terms[(F + f) * 12 * K : (F + f + 1) * 12 * K, columns(block, half)] = low

    bases = local_bases(F, nf)

    def update(source, damping, lanes):
        sums = lax.dot_general(terms[...], hot[lanes, :], (((1,), (1,)), ((), ())),
                               preferred_element_type=jnp.float32)
        half = F * 12 * K
        sums = sums[:half] + sums[half:]
        for f in range(F):
            part = [sums[(f * 12 + c) * K : (f * 12 + c + 1) * K] for c in range(12)]
            old, step = [], []
            for c in range(8):
                prior = from_basis(bases, f, [poly_ref[j, c, :, lanes] for j in range(terms_poly)])
                gain = source[f, c, :, lanes]
                old.append(gain)
                step.append(part[c] - duals_ref[f, c, :, lanes] - RHO * (gain - prior))
            top, bottom, real, imag = part[8:]
            shift = damping * 0.5 * (top + bottom) + RHO
            upper, lower = top + shift, bottom + shift
            scale = 1.0 / (upper * lower - real * real - imag * imag)
            a, d, br, bi = lower * scale, upper * scale, -real * scale, -imag * scale
            sr, si = split(step)
            for row in range(2):
                p, q = 2 * row, 2 * row + 1
                gains_out[f, p, :, lanes] = old[p] + sr[p] * a + sr[q] * br + si[q] * bi
                gains_out[f, p + 4, :, lanes] = old[p + 4] + si[p] * a + si[q] * br - sr[q] * bi
                gains_out[f, q, :, lanes] = old[q] + sr[p] * br - si[p] * bi + sr[q] * d
                gains_out[f, q + 4, :, lanes] = old[q + 4] + si[p] * br + sr[p] * bi + si[q] * d

    def take(block, f):
        if f == 0:
            make_hot(block)
            gather(block)
        rows_sums(block, [f])

    loads[0].wait()
    load_gains(gains_ref[...].reshape(FK, S))
    for f in range(F):
        take(tm, f)
    for f in range(F):
        for d in (1, 3):
            arrived(tm_at(d, 0), f)
            relay(d, f)
    for e in range(1, inner):
        for f in range(F):
            arrived(tm_at(0, e), f)
            take(tm_at(0, e), f)
    for f in range(F):
        arrived(tm_at(2, 0), f)
        relay(2, f)
    for d in (1, 3, 2):
        for f in range(F):
            take(tm_at(d, 0), f)
    for d in (1, 3, 2):
        for e in range(1, inner):
            for f in range(F):
                arrived(tm_at(d, e), f)
                take(tm_at(d, e), f)

    loads[1].wait()
    loads[2].wait()
    update(gains_ref, 12.0, slice(0, S))
    for inner_step in range(1, ITERS):
        load_gains(gains_out[...].reshape(FK, S))

        @pl.loop(0, nt)
        def _(block):
            gather(block)
            rows_sums(block, range(F))

        if inner_step < ITERS - 1:
            update(gains_out, 12.0 * 0.5**inner_step, slice(0, S))

    def fq_copy(owner, chunk, slot, device):
        return pltpu.make_async_remote_copy(
            src_ref=mixed.at[owner, chunk], dst_ref=mixed.at[owner, chunk],
            send_sem=fq_send.at[slot, chunk], recv_sem=fq_recv.at[owner, chunk],
            device_id={"freq": device}, device_id_type=MESH)

    fq_sends = []

    def fq_start(owner, chunk, slot, device):
        copy = fq_copy(owner, chunk, slot, device)
        copy.start()
        fq_sends.append(copy)

    others = nf // 2
    for chunk in range(chunks):
        lanes = slice(chunk * CH, (chunk + 1) * CH)
        update(gains_out, 12.0 * 0.5 ** (ITERS - 1), lanes)
        value = gains_out[:, :, :, lanes] + duals_ref[:, :, :, lanes] * (1.0 / RHO)
        mixed[fq, chunk] = value.reshape(2, FK // 2, CH)
        for d in range(1, others):
            fq_start(fq, chunk, d, (fq + 2 * d) % nf)
        fq_start(fq, chunk, 0, partner)

    for chunk in range(chunks):
        for d in range(1, others):
            owner = (fq - 2 * d + nf) % nf
            fq_copy(owner, chunk, 0, partner).wait_recv()
            fq_start(owner, chunk, others + d, partner)
    for chunk in range(chunks):
        fq_copy(partner, chunk, 0, partner).wait_recv()
        for d in range(1, others):
            fq_copy((partner - 2 * d + nf) % nf, chunk, 0, partner).wait_recv()
    for copy in sends + fq_sends:
        copy.wait_send()


def solution(mesh):
    nt, nf = mesh.shape["tm"], mesh.shape["freq"]

    def shards(visibilities, coherencies, pairs, gains_start, duals_start, poly_start):
        F, _, K, S = gains_start.shape
        inner = nt // OUTER
        chunks = 2
        FK = F * 8 * K
        CH = S // chunks
        cfg = (F, K, S, nt, nf, inner, chunks, poly_start.shape[0])
        like = lambda x: jax.ShapeDtypeStruct(x.shape, jnp.float32)
        vmem = pl.BlockSpec(memory_space=pltpu.VMEM)
        hbm = pl.BlockSpec(memory_space=pltpu.HBM)
        gains, mixed = pl.pallas_call(
            partial(kernel, cfg),
            out_shape=(like(gains_start), jax.ShapeDtypeStruct((nf, chunks, 2, FK // 2, CH), jnp.float32)),
            in_specs=[hbm] * 6,
            out_specs=(vmem,) * 2,
            scratch_shapes=[
                pltpu.VMEM((nt, F, 16 + 8 * K, LANES), jnp.float32),
                pltpu.VMEM((S, nt * 2 * LANES), jnp.bfloat16),
                pltpu.VMEM((2 * F * 12 * K, nt * 2 * LANES), jnp.bfloat16),
                pltpu.VMEM((2 * FK, S), jnp.bfloat16),
                pltpu.VMEM((nt, FK, 2 * LANES), jnp.float32),
                pltpu.VMEM(visibilities.shape, jnp.float32),
                pltpu.VMEM(coherencies.shape, jnp.bfloat16),
                pltpu.VMEM(pairs.shape, jnp.int32),
                pltpu.VMEM(gains_start.shape, jnp.float32),
                pltpu.VMEM(gains_start.shape, jnp.float32),
                pltpu.VMEM(poly_start.shape, jnp.float32),
                pltpu.SemaphoreType.DMA((OUTER + OUTER * inner, F)),
                pltpu.SemaphoreType.DMA((nt, F)),
                pltpu.SemaphoreType.DMA((nf + 1, chunks)),
                pltpu.SemaphoreType.DMA((nf, chunks)),
                pltpu.SemaphoreType.DMA((6,)),
            ],
            compiler_params=pltpu.CompilerParams(collective_id=0, has_side_effects=True,
                                                 vmem_limit_bytes=58 * 2**20),
        )(visibilities, coherencies, pairs, gains_start, duals_start, poly_start)
        own = pl.BlockSpec((F, 8, K, CH), lambda i: (0, 0, 0, i))
        return pl.pallas_call(
            partial(fit_kernel, cfg),
            grid=(chunks,),
            out_shape=(like(gains_start), like(duals_start), like(poly_start)),
            in_specs=[pl.BlockSpec((nf, 1, 2, FK // 2, CH), lambda i: (0, i, 0, 0, 0)), own, own],
            out_specs=(own, own, pl.BlockSpec((poly_start.shape[0], 8, K, CH), lambda i: (0, 0, 0, i))),
            compiler_params=pltpu.CompilerParams(vmem_limit_bytes=60 * 2**20),
        )(mixed, gains, duals_start)

    placed = (
        P("freq", None, "tm"),
        P("freq", None, None, "tm"),
        P(None, "tm"),
        P("freq", None, None, None),
        P("freq", None, None, None),
        P(),
    )
    return jax.shard_map(
        shards,
        mesh=mesh,
        in_specs=placed,
        out_specs=(P("freq", None, None, None), P("freq", None, None, None), P()),
        check_vma=False,
    )
```
